32 devices in a mesh: dp: 8 (over z, y), tensor: 4 (over x, core).
Axes of the slice: x: 2, y: 2, z: 4, core: 2. Of those that a mesh axis runs over, the one named last changes fastest.
Arguments:
- inputs: bfloat16 [16384, 768], P('dp'), may hold values from -6 to 6
- first_values: bfloat16 [16384, 384], P('dp'), may hold values from -6 to 6
- piece_start: int32 [16, 2], P('dp'), may hold values from 0 to 896, as said below
- piece_length: int32 [16, 2], P('dp'), may hold values from 128 to 256, as said below
- cotangent: bfloat16 [16384, 768], P('dp'), may hold values from -6 to 6
- pre_attn_gain: float32 [768], replicated, may hold values from 0.5 to 1.5
- pre_attn_bias: float32 [768], replicated, may hold values from -1.5 to 1.5
- w_query: bfloat16 [768, 768], P(None, 'tensor'), may hold values from -0.21875 to 0.21875
- w_key: bfloat16 [768, 768], P(None, 'tensor'), may hold values from -0.21875 to 0.21875
- w_value: bfloat16 [768, 384], replicated, may hold values from -0.21875 to 0.21875
- w_out: bfloat16 [768, 768], P('tensor'), may hold values from -1.75 to 1.75
- pre_mlp_gain: float32 [768], replicated, may hold values from 0.5 to 1.5
- pre_mlp_bias: float32 [768], replicated, may hold values from -1.5 to 1.5
- w_up: bfloat16 [768, 3072], P(None, 'tensor'), may hold values from -0.21875 to 0.21875
- b_up: float32 [3072], P('tensor'), may hold values from -1.5 to 1.5
- w_down: bfloat16 [3072, 768], P('tensor'), may hold values from -0.109375 to 0.109375
- b_down: float32 [768], replicated, may hold values from -1.5 to 1.5
Outputs:
- outputs: bfloat16 [16384, 768], P('dp')
- grad_inputs: float32 [16384, 768], P('dp')
- grad_first_values: float32 [16384, 384], P('dp')
- grad_pre_attn_gain: float32 [768], replicated
- grad_pre_attn_bias: float32 [768], replicated
- grad_w_query: float32 [768, 768], P(None, 'tensor')
- grad_w_key: float32 [768, 768], P(None, 'tensor')
- grad_w_value: float32 [768, 384], replicated
- grad_w_out: float32 [768, 768], P('tensor')
- grad_pre_mlp_gain: float32 [768], replicated
- grad_pre_mlp_bias: float32 [768], replicated
- grad_w_up: float32 [768, 3072], P(None, 'tensor')
- grad_b_up: float32 [3072], P('tensor')
- grad_w_down: float32 [3072, 768], P('tensor')
- grad_b_down: float32 [768], replicated
The draws below stay inside these ranges and needn't reach their ends.
Inputs may be any that keep to these rules, and one draw needn't show every extreme that they name: `piece_start`: piece p of a sequence lies within tokens p * (512) to (p + 1) * 512 - 1. `piece_length`: the first piece of every sequence has 256 tokens.
All inputs are finite; a program needn't handle non-finite values.
Results may differ from the reference program's by a relative error of at most 0.017.
Values may be sent and summed in bfloat16 or wider, within the bound.
No kernel may reach another device: no remote copies, remote signals or barrier semaphores. Data moves between devices by JAX's collectives and lax.ppermute only.
A program may use at most 128 MiB of HBM per device.

```python
import jax
import jax.numpy as jnp
from jax import lax

D = 768
HEADS = 12
HD = 64
FF = 3072
VF = 384
SEQ_LEN = 1024
PIECE = 256
NPIECE = 2
SEQS = 16
TOKENS = 16384
N_TENSOR = 4


def piece_layout(key):
    span_width = SEQ_LEN // NPIECE
    lengths = jax.random.randint(jax.random.fold_in(key, 11), (SEQS, NPIECE), PIECE // 2, PIECE + 1)
    column = jnp.arange(NPIECE, dtype=jnp.int32)[None, :]
    lengths = jnp.where(column == 0, PIECE, lengths).astype(jnp.int32)
    offsets = jax.random.randint(jax.random.fold_in(key, 12), (SEQS, NPIECE), 0, span_width - lengths + 1)
    starts = offsets + span_width * column
    return (starts.astype(jnp.int32), lengths)


def draw_piece_start(key, part):
    return piece_layout(key)[0]


def draw_piece_length(key, part):
    return piece_layout(key)[1]


def level_of(rng, dims, split, smallest, high):
    level, own = 1.0, jax.random.fold_in(rng, 6)
    for dim, parts in split:
        draws = jnp.exp(jax.random.uniform(jax.random.fold_in(own, dim), (parts,), jnp.float32, smallest / len(split), high / len(split)))
        level = level * jnp.repeat(draws, dims[dim] // parts).reshape([-1 if axis == dim else 1 for axis in range(len(dims))])
    return level


def noise(own_key, extent, spread, reach, shards=(), kind=jnp.bfloat16):
    factor_of = level_of(own_key, extent, shards, -0.22, 0.18) if shards else 1.0
    entries = jax.random.normal(own_key, extent, jnp.float32) * spread * factor_of
    return jnp.minimum(jnp.maximum(entries, -reach), reach).astype(kind)


def setup_inputs(seed: int = 0) -> dict:
    arg_keys = jax.random.split(jax.random.key(seed), 18)
    inputs = noise(arg_keys[0], (TOKENS, D), 1.0, 6.0, ((0, 8),))
    first_values = noise(arg_keys[1], (TOKENS, VF), 1.0, 6.0, ((0, 8),))
    piece_start = draw_piece_start(jax.random.fold_in(arg_keys[17], 71), 0)
    piece_length = draw_piece_length(jax.random.fold_in(arg_keys[17], 71), 0)
    cotangent = noise(arg_keys[4], (TOKENS, D), 1.0, 6.0, ((0, 8),))
    pre_attn_gain = jnp.clip(1.0 + 0.1 * jax.random.normal(arg_keys[5], (D,), jnp.float32), 0.5, 1.5)
    pre_attn_bias = noise(arg_keys[6], (D,), 0.3, 1.5, (), jnp.float32)
    w_query = noise(arg_keys[7], (D, D), D ** -0.5, 0.21875, ((1, 4),))
    w_key = noise(arg_keys[8], (D, D), D ** -0.5, 0.21875, ((1, 4),))
    w_value = noise(arg_keys[9], (D, VF), D ** -0.5, 0.21875)
    w_out = noise(arg_keys[10], (D, D), (max(D // 64, 4)) ** -0.5, 1.75, ((0, 4),))
    pre_mlp_gain = jnp.clip(1.0 + 0.1 * jax.random.normal(arg_keys[11], (D,), jnp.float32), 0.5, 1.5)
    pre_mlp_bias = noise(arg_keys[12], (D,), 0.3, 1.5, (), jnp.float32)
    w_up = noise(arg_keys[13], (D, FF), D ** -0.5, 0.21875, ((1, 4),))
    b_up = noise(arg_keys[14], (FF,), 0.3, 1.5, ((0, 4),), jnp.float32)
    w_down = noise(arg_keys[15], (FF, D), FF ** -0.5, 0.109375, ((0, 4),))
    b_down = noise(arg_keys[16], (D,), 0.3, 1.5, (), jnp.float32)
    return {"inputs": inputs, "first_values": first_values, "piece_start": piece_start, "piece_length": piece_length, "cotangent": cotangent, "pre_attn_gain": pre_attn_gain, "pre_attn_bias": pre_attn_bias, "w_query": w_query, "w_key": w_key, "w_value": w_value, "w_out": w_out, "pre_mlp_gain": pre_mlp_gain, "pre_mlp_bias": pre_mlp_bias, "w_up": w_up, "b_up": b_up, "w_down": w_down, "b_down": b_down}


@jax.custom_vjp
def low(v):
    return lax.optimization_barrier(v.astype(jnp.bfloat16)).astype(jnp.float32)

@jax.custom_vjp
def low_back(v):
    return v

def low_keep(v):
    return (low(v), None)

def low_pass(kept, grad):
    return (grad,)

def back_keep(v):
    return (v, None)

def back_low(kept, grad):
    return (low(grad),)
low.defvjp(low_keep, low_pass)
low_back.defvjp(back_keep, back_low)
highest = lax.Precision.HIGHEST

def normalize(values, norm_gain, norm_shift):
    centered = values - lax.optimization_barrier(jnp.mean(values, axis=-1, keepdims=True))
    inverse = lax.rsqrt(lax.optimization_barrier(jnp.mean(centered * centered, axis=-1, keepdims=True)) + 1e-05)
    return centered * inverse * norm_gain + norm_shift

def piece_labels(starts, lengths):
    places = jnp.arange(SEQ_LEN, dtype=jnp.int32)
    inside = (places[None, None, :] >= starts[:, :, None]) & (places[None, None, :] < (starts + lengths)[:, :, None])
    numbers = jnp.arange(1, NPIECE + 1, dtype=jnp.int32)
    return lax.optimization_barrier(jnp.sum(jnp.where(inside, numbers[None, :, None], 0), axis=1)).astype(jnp.int32)

def by_heads(matrix):
    return matrix.reshape(SEQ_LEN, HEADS, HD)

def attend(operands):
    queries, keys_all, values_all, labels = operands
    places = jnp.arange(SEQ_LEN, dtype=jnp.int32)
    allowed = (places[None, :] <= places[:, None]) | (labels[:, None] == labels[None, :]) & (labels[:, None] > 0)
    scores = jnp.einsum('qhe,khe->hqk', by_heads(queries), by_heads(keys_all), precision=highest) * 0.125
    scores = low_back(scores)
    scores = jnp.where(allowed[None], scores, -1e+30)
    attn_probs = low(jax.nn.softmax(scores, axis=-1))
    mixed = jnp.einsum('hqk,khe->qhe', attn_probs, by_heads(values_all), precision=highest)
    return mixed.reshape(SEQ_LEN, D)

def layer(seq_inputs, seq_firsts, seq_labels, attn_gain, attn_shift, query_w, key_w, value_w, out_w, mlp_gain, mlp_shift, up_w, up_bias, down_w, down_bias):
    group_size = seq_inputs.shape[0]
    attn_in = low(normalize(seq_inputs, attn_gain, attn_shift))
    queries = low_back(low(jnp.einsum('gld,de->gle', attn_in, query_w, precision=highest)))
    keys_all = low_back(low(jnp.einsum('gld,de->gle', attn_in, key_w, precision=highest)))
    fresh = low_back(low(jnp.einsum('gld,de->gle', attn_in, value_w, precision=highest)))
    values_all = jnp.concatenate([fresh, seq_firsts], axis=-1)
    mixed_heads = lax.map(jax.checkpoint(attend), (queries, keys_all, values_all, seq_labels))
    mixed_heads = low_back(low(mixed_heads))
    head_terms = jnp.einsum('gltk,tkd->gltd', mixed_heads.reshape(group_size, SEQ_LEN, N_TENSOR, D // N_TENSOR), out_w.reshape(N_TENSOR, D // N_TENSOR, D), precision=highest)
    attn_out = low_back(lax.optimization_barrier(jnp.sum(low(head_terms), axis=2)))
    hidden = seq_inputs + attn_out
    mlp_in = low(normalize(hidden, mlp_gain, mlp_shift))
    pre_act = low_back(jnp.einsum('gld,df->glf', mlp_in, up_w, precision=highest) + up_bias)
    active = low(jax.nn.gelu(pre_act, approximate=True))
    unit_terms = jnp.einsum('gltf,tfd->gltd', active.reshape(group_size, SEQ_LEN, N_TENSOR, FF // N_TENSOR), down_w.reshape(N_TENSOR, FF // N_TENSOR, D), precision=highest)
    return hidden + lax.optimization_barrier(jnp.sum(low(unit_terms), axis=2)) + down_bias

def reference(inputs, first_values, piece_start, piece_length, cotangent, pre_attn_gain, pre_attn_bias, w_query, w_key, w_value, w_out, pre_mlp_gain, pre_mlp_bias, w_up, b_up, w_down, b_down):
    group_size = min(SEQS, max(1, 4096 // SEQ_LEN))
    steps_count = SEQS // group_size
    seq_inputs = inputs.astype(jnp.float32).reshape(steps_count, group_size, SEQ_LEN, D)
    seq_firsts = first_values.astype(jnp.float32).reshape(steps_count, group_size, SEQ_LEN, VF)
    seq_cots = cotangent.astype(jnp.float32).reshape(steps_count, group_size, SEQ_LEN, D)
    labels_all = piece_labels(piece_start, piece_length).reshape(steps_count, group_size, SEQ_LEN)
    params = (pre_attn_gain.astype(jnp.float32), pre_attn_bias.astype(jnp.float32), w_query.astype(jnp.float32), w_key.astype(jnp.float32), w_value.astype(jnp.float32), w_out.astype(jnp.float32), pre_mlp_gain.astype(jnp.float32), pre_mlp_bias.astype(jnp.float32), w_up.astype(jnp.float32), b_up.astype(jnp.float32), w_down.astype(jnp.float32), b_down.astype(jnp.float32))

    def step(totals, slices):
        group_inputs, group_firsts, group_labels, group_cots = slices

        def forward(xin, fin, *weights):
            return layer(xin, fin, group_labels, *weights)
        result, pullback = jax.vjp(forward, group_inputs, group_firsts, *params)
        gradients = pullback(group_cots)
        totals = tuple((acc + new for acc, new in zip(totals, gradients[2:])))
        return (totals, (result.astype(jnp.bfloat16), gradients[0], gradients[1]))
    start_totals = tuple((jnp.zeros_like(weight) for weight in params))
    totals, (outs_all, grad_in, grad_first) = lax.scan(step, start_totals, (seq_inputs, seq_firsts, labels_all, seq_cots))
    return (outs_all.reshape(TOKENS, D), grad_in.reshape(TOKENS, D), grad_first.reshape(TOKENS, VF), totals[0], totals[1], totals[2], totals[3], totals[4], totals[5], totals[6], totals[7], totals[8], totals[9], totals[10], totals[11])
```

```python
from functools import partial

import jax
import jax.numpy as jnp
from jax import lax
from jax.experimental import pallas as pl
from jax.experimental.pallas import tpu as pltpu
from jax.sharding import PartitionSpec as P

HEADS = 12
HD = 64
VFRESH = 6

score_scale = 0.125
far_below = -1e30
epsilon = 1e-05

F32 = jnp.float32
BF16 = jnp.bfloat16
VMEM_BYTES = 56 << 20


def nn(left, right):
    return lax.dot_general(left, right, (((1,), (0,)), ((), ())), preferred_element_type=F32)


def nt(left, right):
    return lax.dot_general(left, right, (((1,), (1,)), ((), ())), preferred_element_type=F32)


def tn(left, right):
    return lax.dot_general(left, right, (((0,), (0,)), ((), ())), preferred_element_type=F32)


def normal_parts(values):
    centered = values - jnp.mean(values, axis=-1, keepdims=True)
    inverse = lax.rsqrt(jnp.mean(centered * centered, axis=-1, keepdims=True) + epsilon)
    return centered * inverse, inverse


def norm_pull(upstream, normal_part, inverse, norm_gain):
    scaled = upstream * norm_gain
    return inverse * (
        scaled
        - jnp.mean(scaled, axis=-1, keepdims=True)
        - normal_part * jnp.mean(scaled * normal_part, axis=-1, keepdims=True)
    )


def whole(shape):
    return pl.BlockSpec(shape, lambda *_: (0,) * len(shape))


def shaped(shape, dtype):
    return jax.ShapeDtypeStruct(shape, dtype)


def params(**more):
    return pltpu.CompilerParams(vmem_limit_bytes=VMEM_BYTES, **more)


def project_body(fresh, x_ref, gain_ref, shift_ref, wq_ref, wk_ref, wv_ref, first_ref, low_ref, q_ref, k_ref, v_ref):
    normal, _ = normal_parts(x_ref[...].astype(F32))
    low = (normal * gain_ref[...] + shift_ref[...]).astype(BF16)
    low_ref[...] = low
    q_ref[...] = nn(low, wq_ref[...]).astype(BF16)
    k_ref[...] = nn(low, wk_ref[...]).astype(BF16)

    @pl.when(fresh[0] == 1)
    def _():
        v_ref[...] = nn(low, wv_ref[...]).astype(BF16)

    @pl.when(fresh[0] == 0)
    def _():
        v_ref[...] = first_ref[...]


def project(fresh, x, gain, shift, wq, wk, wv, first, seq, length, rows=256):
    width, cols = wq.shape
    steps = length // rows
    at = lambda i, *_: (seq * steps + i, 0)
    out = lambda i, *_: (i, 0)
    return pl.pallas_call(
        project_body,
        out_shape=(shaped((length, width), BF16),) + (shaped((length, cols), BF16),) * 3,
        grid_spec=pltpu.PrefetchScalarGridSpec(
            num_scalar_prefetch=1,
            grid=(steps,),
            in_specs=[
                pl.BlockSpec((rows, width), at),
                whole((1, width)),
                whole((1, width)),
                whole((width, cols)),
                whole((width, cols)),
                whole((width, cols)),
                pl.BlockSpec((rows, cols), at),
            ],
            out_specs=(pl.BlockSpec((rows, width), out),) + (pl.BlockSpec((rows, cols), out),) * 3,
        ),
        compiler_params=params(),
        name="project",
    )(fresh, x, gain, shift, wq, wk, wv, first)


def span_bias(start, size, base, keys, rows, row0):
    key_pos = base + lax.broadcasted_iota(jnp.int32, (keys, rows), 0)
    query_pos = base + row0 + lax.broadcasted_iota(jnp.int32, (keys, rows), 1)
    stop = start + size
    both = (key_pos >= start) & (key_pos < stop) & (query_pos >= start) & (query_pos < stop)
    return jnp.where((key_pos <= query_pos) | both, 0.0, far_below)


def in_tile(part, head, width):
    if width == HD:
        return part
    zero = jnp.zeros_like(part)
    return jnp.concatenate([part, zero] if head % 2 == 0 else [zero, part], 0)


def store_half(side, half, rows, value, own_ref, other_ref):
    @pl.when(side == half)
    def _():
        own_ref[rows, :] = value

    @pl.when(side != half)
    def _():
        other_ref[rows, :] = value


def attend_body(
    side, start, size, q_ref, k_ref, v_ref, wo_ref, zt_ref, lse_ref, own_ref, other_ref, bias_ref, *, heads, span, rb, seq
):
    length = q_ref.shape[0]
    lanes = heads * HD
    half = length // 2
    vt = v_ref[...].T
    qt = (q_ref[...] * score_scale).T
    for p in range(length // span):
        for r in range(0, span, rb):
            bias_ref[:, r : r + rb] = span_bias(start[seq, p], size[seq, p], p * span, span, rb, r)
        before = p * span
        keys = before + span
        for r in range(0, span, rb):
            row0 = before + r
            outs = []
            for h in range(heads):
                lo = h // 2 * 2 * HD
                hi = min(lo + 2 * HD, lanes)
                qh = in_tile(qt[h * HD : (h + 1) * HD, row0 : row0 + rb], h, hi - lo)
                vth = vt[h * HD : (h + 1) * HD, :]
                scores = nn(k_ref[:keys, lo:hi], qh)
                diag = scores[before:] + bias_ref[:, r : r + rb]
                peak = jnp.max(diag, axis=0, keepdims=True)
                if p:
                    peak = jnp.maximum(peak, jnp.max(scores[:before], axis=0, keepdims=True))
                raw = jnp.exp(diag - peak)
                total = jnp.sum(raw, axis=0, keepdims=True)
                zt = nn(vth[:, before:keys], raw.astype(BF16))
                if p:
                    raw = jnp.exp(scores[:before] - peak)
                    total = total + jnp.sum(raw, axis=0, keepdims=True)
                    zt = zt + nn(vth[:, :before], raw.astype(BF16))
                outs.append((zt / total).astype(BF16))
                lse_ref[h : h + 1, row0 : row0 + rb] = peak + jnp.log(total)
            zt = jnp.concatenate(outs, 0)
            zt_ref[:, row0 : row0 + rb] = zt
            out = nn(zt.T, wo_ref[...]).astype(BF16)
            at = row0 % half
            store_half(side[0], row0 // half, slice(at, at + rb), out, own_ref, other_ref)


def attend(side, start, size, q, k, v, wo, heads, seq, rb=512):
    length, lanes = q.shape
    width = wo.shape[1]
    span = length // start.shape[1]
    rb = min(rb, span, length // 2)
    return pl.pallas_call(
        partial(attend_body, heads=heads, span=span, rb=rb, seq=seq),
        out_shape=(
            shaped((lanes, length), BF16),
            shaped((heads, length), F32),
            shaped((length // 2, width), BF16),
            shaped((length // 2, width), BF16),
        ),
        grid_spec=pltpu.PrefetchScalarGridSpec(
            num_scalar_prefetch=3,
            grid=(1,),
            in_specs=[whole(q.shape), whole(q.shape), whole(q.shape), whole(wo.shape)],
            out_specs=(
                whole((lanes, length)),
                whole((heads, length)),
                whole((length // 2, width)),
                whole((length // 2, width)),
            ),
            scratch_shapes=[pltpu.VMEM((span, span), F32)],
        ),
        compiler_params=params(),
        name="attend",
    )(side, start, size, q, k, v, wo)


def attend_pull_body(
    side, start, size, q_ref, k_ref, v_ref, wo_ref, zt_ref, lse_ref, own_in, other_in, low_ref,
    wq_ref, wk_ref, wv_ref, *rest, heads, span, rb, seq, last,
):
    if last:
        old_q, old_k, old_v, old_o = rest[:4]
        rest = rest[4:]
    own_ref, other_ref, dv_ref, gq_ref, gk_ref, gv_ref, go_ref, bias_ref, dk_sum, dv_sum, dqt_ref, dh_ref = rest
    length = q_ref.shape[0]
    lanes = heads * HD
    half = length // 2
    first = side[0] == 0
    dh_ref[:half, :] = jnp.where(first, own_in[...], other_in[...])
    dh_ref[half:, :] = jnp.where(first, other_in[...], own_in[...])
    dz = nt(dh_ref[...], wo_ref[...]).astype(BF16)
    dzt = dz.T
    q = q_ref[...] * score_scale
    qt = q.T
    kt = k_ref[...].T
    low_lane = lax.broadcasted_iota(jnp.int32, (1, 2 * HD), 1) < HD
    dk_sum[...] = jnp.zeros_like(dk_sum)
    dv_sum[...] = jnp.zeros_like(dv_sum)
    for p in range(length // span):
        for r in range(0, span, rb):
            bias_ref[:, r : r + rb] = span_bias(start[seq, p], size[seq, p], p * span, span, rb, r)
        before = p * span
        keys = before + span
        for r in range(0, span, rb):
            row0 = before + r
            dqs = []
            for lo in range(0, lanes, 2 * HD):
                hi = min(lo + 2 * HD, lanes)
                dks = []
                dvs = []
                for h in range(lo // HD, hi // HD):
                    qh = in_tile(qt[h * HD : (h + 1) * HD, row0 : row0 + rb], h, hi - lo)
                    dzh = in_tile(dzt[h * HD : (h + 1) * HD, row0 : row0 + rb], h, hi - lo)
                    lse = lse_ref[h : h + 1, row0 : row0 + rb]
                    scores = nn(k_ref[:keys, lo:hi], qh)
                    dprob = nn(v_ref[:keys, lo:hi], dzh)
                    prob = jnp.exp(scores[before:] + bias_ref[:, r : r + rb] - lse)
                    both = prob * dprob[before:]
                    delta = jnp.sum(both, axis=0, keepdims=True)
                    if p:
                        prob2 = jnp.exp(scores[:before] - lse)
                        both2 = prob2 * dprob[:before]
                        delta = delta + jnp.sum(both2, axis=0, keepdims=True)
                        prob_low = jnp.concatenate([prob2.astype(BF16), prob.astype(BF16)], 0)
                        ds = jnp.concatenate(
                            [(both2 - prob2 * delta).astype(BF16), (both - prob * delta).astype(BF16)], 0
                        )
                    else:
                        prob_low = prob.astype(BF16)
                        ds = (both - prob * delta).astype(BF16)
                    dqs.append((nn(kt[h * HD : (h + 1) * HD, :keys], ds) * score_scale).astype(BF16))
                    dks.append(nn(ds, q[row0 : row0 + rb, lo:hi]))
                    dvs.append(nn(prob_low, dz[row0 : row0 + rb, lo:hi]))
                if len(dks) == 2:
                    dk_sum[:keys, lo:hi] += jnp.where(low_lane, dks[0], dks[1])
                    dv_sum[:keys, lo:hi] += jnp.where(low_lane, dvs[0], dvs[1])
                else:
                    dk_sum[:keys, lo:hi] += dks[0]
                    dv_sum[:keys, lo:hi] += dvs[0]
            dqt_ref[:, row0 : row0 + rb] = jnp.concatenate(dqs, 0)
    dqt = dqt_ref[...]
    dk = dk_sum[...].astype(BF16)
    dv = dv_sum[...].astype(BF16)
    dv_ref[...] = dv
    dx = (nt(dqt.T, wq_ref[...]) + nt(dk, wk_ref[...]) + nt(dv, wv_ref[...])).astype(BF16)
    for part in range(2):
        store_half(side[0], part, slice(0, half), dx[part * half : (part + 1) * half], own_ref, other_ref)
    low = low_ref[...]
    gq = nn(dqt, low)
    gk = nn(dk.T, low)
    gv = nn(dv.T, low)
    go = nn(zt_ref[...], dh_ref[...])
    if last:
        gq_ref[...] = (gq + old_q[...]).T.astype(BF16)
        gk_ref[...] = (gk + old_k[...]).T.astype(BF16)
        gv_ref[...] = (gv + old_v[...]).T.astype(BF16)
        go_ref[...] = (go + old_o[...]).astype(BF16)
    else:
        gq_ref[...] = gq
        gk_ref[...] = gk
        gv_ref[...] = gv
        go_ref[...] = go


def attend_pull(side, start, size, q, k, v, wo, zt, lse, own, other, low, wq, wk, wv, old, heads, seq, last, rb=256):
    length, lanes = q.shape
    width = wo.shape[1]
    span = length // start.shape[1]
    rb = min(rb, span)
    ins = (q, k, v, wo, zt, lse, own, other, low, wq, wk, wv) + tuple(old)
    turned = (width, lanes) if last else (lanes, width)
    kind = BF16 if last else F32
    outs = (
        shaped(own.shape, BF16),
        shaped(own.shape, BF16),
        shaped((length, lanes), BF16),
        shaped(turned, kind),
        shaped(turned, kind),
        shaped(turned, kind),
        shaped((lanes, width), kind),
    )
    return pl.pallas_call(
        partial(attend_pull_body, heads=heads, span=span, rb=rb, seq=seq, last=last),
        out_shape=outs,
        grid_spec=pltpu.PrefetchScalarGridSpec(
            num_scalar_prefetch=3,
            grid=(1,),
            in_specs=[whole(i.shape) for i in ins],
            out_specs=tuple(whole(o.shape) for o in outs),
            scratch_shapes=[
                pltpu.VMEM((span, span), F32),
                pltpu.VMEM((length, lanes), F32),
                pltpu.VMEM((length, lanes), F32),
                pltpu.VMEM((lanes, length), BF16),
                pltpu.VMEM((length, width), BF16),
            ],
        ),
        compiler_params=params(),
        name="attend_pull",
    )(side, start, size, *ins)


def row_call(body, side, ins, outs, sums, seq, rows, name):
    half = next(array.shape[0] for array, kind in ins if kind == "half")
    steps = half // rows
    specs = []
    for array, kind in ins:
        if kind == "half":
            specs.append(pl.BlockSpec((rows, array.shape[1]), lambda i, s: (i, 0)))
        elif kind == "all":
            specs.append(
                pl.BlockSpec((rows, array.shape[1]), lambda i, s: ((2 * seq + s[0]) * steps + i, 0))
            )
        else:
            specs.append(whole(array.shape))
    out_specs = [pl.BlockSpec((rows, o.shape[1]), lambda i, s: (i, 0)) for o in outs]
    out_specs += [whole(o.shape) for o in sums]
    return pl.pallas_call(
        body,
        out_shape=tuple(outs) + tuple(sums),
        grid_spec=pltpu.PrefetchScalarGridSpec(
            num_scalar_prefetch=1, grid=(steps,), in_specs=specs, out_specs=tuple(out_specs)
        ),
        compiler_params=params(),
        name=name,
    )(side, *[array for array, _ in ins])


def norm_mid_body(side, part_ref, got_ref, x_ref, gain_ref, shift_ref, hidden_ref, low_ref):
    hidden = x_ref[...].astype(F32) + (part_ref[...].astype(F32) + got_ref[...].astype(F32))
    hidden_ref[...] = hidden
    normal, _ = normal_parts(hidden)
    low_ref[...] = (normal * gain_ref[...] + shift_ref[...]).astype(BF16)


def add_sums(sum_ref, values):
    @pl.when(pl.program_id(0) == 0)
    def _():
        sum_ref[...] = jnp.zeros_like(sum_ref)

    for row, value in enumerate(values):
        sum_ref[row : row + 1, :] += jnp.sum(value, axis=0, keepdims=True)


def norm_mid_pull_body(side, part_ref, got_ref, hidden_ref, cot_ref, gain_ref, dhidden_ref, low_ref, sum_ref):
    upstream = part_ref[...].astype(F32) + got_ref[...].astype(F32)
    normal, inverse = normal_parts(hidden_ref[...])
    cot = cot_ref[...].astype(F32)
    dhidden = cot + norm_pull(upstream, normal, inverse, gain_ref[...])
    dhidden_ref[...] = dhidden
    low_ref[...] = dhidden.astype(BF16)
    add_sums(sum_ref, (upstream * normal, upstream, cot))


def norm_first_pull_body(side, part_ref, got_ref, dhidden_ref, x_ref, gain_ref, out_ref, sum_ref):
    upstream = part_ref[...].astype(F32) + got_ref[...].astype(F32)
    normal, inverse = normal_parts(x_ref[...].astype(F32))
    out_ref[...] = dhidden_ref[...] + norm_pull(upstream, normal, inverse, gain_ref[...])
    add_sums(sum_ref, (upstream * normal, upstream))


def feed_body(side, x_ref, cot_ref, up_ref, bias_ref, down_ref, dx_ref, out_ref, active_ref, dpre_ref, sum_ref):
    pre = nn(x_ref[...], up_ref[...]) + bias_ref[...]
    root = 0.7978845608028654
    squared = pre * pre
    inner = jnp.tanh(root * pre * (1.0 + 0.044715 * squared))
    rise = 0.5 * (1.0 + inner)
    active = (pre * rise).astype(BF16)
    active_ref[...] = active
    slope = rise + 0.5 * pre * (1.0 - inner * inner) * (root * (1.0 + 3 * 0.044715 * squared))
    dpre = (nt(cot_ref[...], down_ref[...]) * slope).astype(BF16)
    dpre_ref[...] = dpre
    dx_ref[...] = nt(dpre, up_ref[...]).astype(BF16)
    out_ref[...] = nn(active, down_ref[...]).astype(BF16)
    add_sums(sum_ref, (dpre.astype(F32),))


def feed(side, x, cotangent, up, bias, down, seq, flip, rows=256):
    half, width = x.shape
    units = up.shape[1]
    steps = half // rows
    at = lambda i, s: (i, 0)
    if flip:
        cot_at = lambda i, s: ((2 * seq + 1 - s[0]) * steps + i, 0)
    else:
        cot_at = lambda i, s: ((2 * seq + s[0]) * steps + i, 0)
    return pl.pallas_call(
        feed_body,
        out_shape=(
            shaped((half, width), BF16),
            shaped((half, width), BF16),
            shaped((half, units), BF16),
            shaped((half, units), BF16),
            shaped((1, units), F32),
        ),
        grid_spec=pltpu.PrefetchScalarGridSpec(
            num_scalar_prefetch=1,
            grid=(steps,),
            in_specs=[
                pl.BlockSpec((rows, width), at),
                pl.BlockSpec((rows, width), cot_at),
                whole(up.shape),
                whole(bias.shape),
                whole(down.shape),
            ],
            out_specs=(
                pl.BlockSpec((rows, width), at),
                pl.BlockSpec((rows, width), at),
                pl.BlockSpec((rows, units), at),
                pl.BlockSpec((rows, units), at),
                whole((1, units)),
            ),
        ),
        compiler_params=params(),
        name="feed",
    )(side, x, cotangent, up, bias, down)


def outer_body(side, *refs, count):
    total = tn(refs[0][...], refs[count][...])
    for i in range(1, count):
        total = total + tn(refs[i][...], refs[count + i][...])
    refs[-1][...] = total.astype(BF16)


def outer_sum(side, lefts, rights, half, places=None):
    count = len(lefts)
    rows = lefts[0].shape[1]
    cols = rights[0].shape[1]
    specs = [whole(a.shape) for a in lefts]
    for i, array in enumerate(rights):
        if places is None:
            specs.append(whole(array.shape))
        else:
            seq, flip = places[i]
            if flip:
                specs.append(pl.BlockSpec((half, cols), lambda _, s, seq=seq: (2 * seq + 1 - s[0], 0)))
            else:
                specs.append(pl.BlockSpec((half, cols), lambda _, s, seq=seq: (2 * seq + s[0], 0)))
    return pl.pallas_call(
        partial(outer_body, count=count),
        out_shape=shaped((rows, cols), BF16),
        grid_spec=pltpu.PrefetchScalarGridSpec(
            num_scalar_prefetch=1, grid=(1,), in_specs=specs, out_specs=whole((rows, cols))
        ),
        compiler_params=params(),
        name="outer_sum",
    )(side, *lefts, *rights)


def xor_pairs(size, bit):
    return [(i, i ^ bit) for i in range(size)]


def xor_sum(value, axis):
    size = lax.axis_size(axis)
    bit = 1
    while bit < size:
        value = value + lax.ppermute(value, axis, xor_pairs(size, bit))
        bit *= 2
    return value


def on_device(
    inputs,
    first_values,
    piece_start,
    piece_length,
    cotangent,
    pre_attn_gain,
    pre_attn_bias,
    w_query,
    w_key,
    w_value,
    w_out,
    pre_mlp_gain,
    pre_mlp_bias,
    w_up,
    b_up,
    w_down,
    b_down,
):
    groups = lax.axis_size("tensor")
    member = lax.axis_index("tensor")
    local_heads = HEADS // groups
    columns = local_heads * HD
    is_fresh = member < VFRESH // local_heads
    core = member % 2
    tokens_dev, width = inputs.shape
    value_width = w_value.shape[1]
    seq_count = piece_start.shape[0]
    length = tokens_dev // seq_count
    half = length // 2
    side = core.astype(jnp.int32).reshape(1)
    fresh = is_fresh.astype(jnp.int32).reshape(1)
    seqs = range(seq_count)
    near = partial(lax.ppermute, axis_name="tensor", perm=xor_pairs(groups, 1))
    far = partial(lax.ppermute, axis_name="tensor", perm=xor_pairs(groups, 2))

    def row(vector):
        return vector.reshape(1, -1)

    def reduce_start(own, other):
        part = (own.astype(F32) + near(other).astype(F32)).astype(BF16)
        return part, far(part)

    def spread(own):
        got = near(own)
        return jnp.where(core == 0, own, got), jnp.where(core == 0, got, own)

    gain1, shift1, gain2, shift2 = map(row, (pre_attn_gain, pre_attn_bias, pre_mlp_gain, pre_mlp_bias))
    value_cols = lax.dynamic_slice_in_dim(
        w_value, jnp.minimum(member * columns, value_width - columns), columns, 1
    )
    first_cols = lax.dynamic_slice_in_dim(
        first_values, jnp.maximum(member * columns - value_width, 0), columns, 1
    )
    value_back = jnp.where(is_fresh, value_cols, jnp.zeros_like(value_cols))

    low, q, k, v, zt, lse, attn_part = [], [], [], [], [], [], []
    for s in seqs:
        a, b, c, d = project(
            fresh, inputs, gain1, shift1, w_query, w_key, value_cols, first_cols, s, length
        )
        low.append(a), q.append(b), k.append(c), v.append(d)
        z, l, own, other = attend(side, piece_start, piece_length, b, c, d, w_out, local_heads, s)
        zt.append(z), lse.append(l)
        attn_part.append(reduce_start(own, other))

    hidden, acts, dpres, mids, places, mlp_part, dmid_part, up_sums = [], [], [], [], [], [], [], []
    for s in seqs:
        part, got = attn_part[s]
        h, mid = row_call(
            norm_mid_body,
            side,
            [(part, "half"), (got, "half"), (inputs, "all"), (gain2, "vector"), (shift2, "vector")],
            [shaped((half, width), F32), shaped((half, width), BF16)],
            [],
            s,
            128,
            "norm_mid",
        )
        hidden.append(h)
        pieces = []
        for flip, piece in enumerate((mid, near(mid))):
            dx, out, act, dpre, sums = feed(
                side, piece, cotangent, w_up, row(b_up), w_down, s, flip
            )
            mids.append(piece), acts.append(act), dpres.append(dpre), places.append((s, flip))
            pieces.append((dx, out))
            up_sums.append(sums)
        dmid_part.append(reduce_start(pieces[0][0], pieces[1][0]))
        mlp_part.append((pieces[0][1], pieces[1][1]))

    grad_w_down = outer_sum(side, acts, [cotangent] * len(acts), half, places)
    grad_w_up = outer_sum(side, mids, dpres, half)
    grad_b_up = sum(up_sums)[0]

    dhidden, mid_sums, dlow, value_parts, in_part = [], [], [], [], []
    grads = ()
    for s in seqs:
        part, got = dmid_part[s]
        dh, dlo, sums = row_call(
            norm_mid_pull_body,
            side,
            [(part, "half"), (got, "half"), (hidden[s], "half"), (cotangent, "all"), (gain2, "vector")],
            [shaped((half, width), F32), shaped((half, width), BF16)],
            [shaped((3, width), F32)],
            s,
            128,
            "norm_mid_pull",
        )
        dhidden.append(dh), mid_sums.append(sums)
        own, other, dv, *grads = attend_pull(
            side, piece_start, piece_length, q[s], k[s], v[s], w_out, zt[s], lse[s], dlo, near(dlo), low[s],
            w_query, w_key, value_back, grads, local_heads, s, s == seq_count - 1,
        )
        value_parts.append(dv)
        in_part.append(reduce_start(own, other))

    outputs = []
    for s in seqs:
        part, got = reduce_start(*mlp_part[s])
        out = (hidden[s] + (part.astype(F32) + got.astype(F32)) + b_down).astype(BF16)
        outputs.extend(spread(out))
    outputs = jnp.concatenate(outputs, 0)

    grad_inputs, first_sums = [], []
    for s in seqs:
        part, got = in_part[s]
        g, sums = row_call(
            norm_first_pull_body,
            side,
            [(part, "half"), (got, "half"), (dhidden[s], "half"), (inputs, "all"), (gain1, "vector")],
            [shaped((half, width), F32)],
            [shaped((2, width), F32)],
            s,
            128,
            "norm_first_pull",
        )
        first_sums.append(sums)
        grad_inputs.extend(spread(g))
    grad_inputs = jnp.concatenate(grad_inputs, 0)

    fresh_members = VFRESH // local_heads
    firsts = []
    for s in seqs:
        got = lax.ppermute(
            value_parts[s], "tensor", [(i + fresh_members, i) for i in range(groups - fresh_members)]
        )
        mine = jnp.where(is_fresh, got, value_parts[s])
        got = near(mine)
        firsts.append(
            jnp.concatenate([jnp.where(core == 0, mine, got), jnp.where(core == 0, got, mine)], 1)
        )
    grad_first_values = jnp.concatenate(firsts, 0).astype(F32)

    grad_w_down, grad_w_up = lax.psum((grad_w_down, grad_w_up), "dp")
    grads, _ = lax.optimization_barrier((tuple(grads), grad_w_up[0, 0]))
    gq, gk, gv, go = lax.psum(grads, "dp")
    got = lax.ppermute(gv, "tensor", [(i, i + fresh_members) for i in range(groups - fresh_members)])
    mine = jnp.where(is_fresh, gv, got)
    got = near(mine)
    grad_w_value = jnp.concatenate(
        [jnp.where(core == 0, mine, got), jnp.where(core == 0, got, mine)], 1
    ).astype(F32)

    shared = jnp.concatenate([sum(first_sums), sum(mid_sums)], 0)
    shared = shared + near(shared)
    small = xor_sum(jnp.concatenate([shared, row(grad_b_up)], 0), "dp")

    return (
        outputs,
        grad_inputs,
        grad_first_values,
        small[0],
        small[1],
        gq.astype(F32),
        gk.astype(F32),
        grad_w_value,
        go.astype(F32),
        small[2],
        small[3],
        grad_w_up.astype(F32),
        small[5],
        grad_w_down.astype(F32),
        small[4],
    )


def solution(mesh):
    return jax.shard_map(
        on_device,
        mesh=mesh,
        in_specs=(
            P("dp", None),
            P("dp", None),
            P("dp", None),
            P("dp", None),
            P("dp", None),
            P(),
            P(),
            P(None, "tensor"),
            P(None, "tensor"),
            P(),
            P("tensor", None),
            P(),
            P(),
            P(None, "tensor"),
            P("tensor"),
            P("tensor", None),
            P(),
        ),
        out_specs=(
            P("dp", None),
            P("dp", None),
            P("dp", None),
            P(),
            P(),
            P(None, "tensor"),
            P(None, "tensor"),
            P(),
            P("tensor", None),
            P(),
            P(),
            P(None, "tensor"),
            P("tensor"),
            P("tensor", None),
            P(),
        ),
        check_vma=False,
    )
```

```python
from functools import partial

import jax
import jax.numpy as jnp
from jax import lax
from jax.experimental import pallas as pl
from jax.experimental.pallas import tpu as pltpu
from jax.sharding import PartitionSpec as P

HEADS = 12
HD = 64
VFRESH = 6

score_scale = 0.125
far_below = -1e30
epsilon = 1e-05

F32 = jnp.float32
BF16 = jnp.bfloat16
VMEM_BYTES = 56 << 20


def nn(left, right):
    return lax.dot_general(left, right, (((1,), (0,)), ((), ())), preferred_element_type=F32)


def nt(left, right):
    return lax.dot_general(left, right, (((1,), (1,)), ((), ())), preferred_element_type=F32)


def tn(left, right):
    return lax.dot_general(left, right, (((0,), (0,)), ((), ())), preferred_element_type=F32)


def normal_parts(values):
    centered = values - jnp.mean(values, axis=-1, keepdims=True)
    inverse = lax.rsqrt(jnp.mean(centered * centered, axis=-1, keepdims=True) + epsilon)
    return centered * inverse, inverse


def norm_pull(upstream, normal_part, inverse, norm_gain):
    scaled = upstream * norm_gain
    return inverse * (
        scaled
        - jnp.mean(scaled, axis=-1, keepdims=True)
        - normal_part * jnp.mean(scaled * normal_part, axis=-1, keepdims=True)
    )


def whole(shape):
    return pl.BlockSpec(shape, lambda *_: (0,) * len(shape))


def shaped(shape, dtype):
    return jax.ShapeDtypeStruct(shape, dtype)


def params(**more):
    return pltpu.CompilerParams(vmem_limit_bytes=VMEM_BYTES, **more)


CHIP = 4
CORE = 5


def project_body(place, x_ref, vec_ref, wq_ref, wk_ref, wv_ref, first_ref, low_ref, q_ref, k_ref, own_ref, far_ref):
    normal, _ = normal_parts(x_ref[...].astype(F32))
    low = (normal * vec_ref[0:1, :] + vec_ref[1:2, :]).astype(BF16)
    low_ref[...] = low
    q_ref[...] = nt(low, wq_ref[...]).astype(BF16)
    k_ref[...] = nt(low, wk_ref[...]).astype(BF16)
    cols = q_ref.shape[1]
    fresh = nn(low, wv_ref[...]).astype(BF16)
    left = place[CORE] == 0
    fresh = jnp.where(left, fresh[:, :cols], fresh[:, cols:])
    first = jnp.where(left, first_ref[:, :cols], first_ref[:, cols:])
    own_fresh = place[CHIP] == 0
    own_ref[...] = jnp.where(own_fresh, fresh, first)
    far_ref[...] = jnp.where(own_fresh, first, fresh)


def project(place, x, vecs, wq, wk, wv, first, length, rows=256):
    cols, width = wq.shape
    steps = length // rows
    at = lambda i, s: (s[CHIP] * steps + i, 0)
    out = lambda i, s: (i, 0)
    return pl.pallas_call(
        project_body,
        out_shape=(shaped((length, width), BF16),) + (shaped((length, cols), BF16),) * 4,
        grid_spec=pltpu.PrefetchScalarGridSpec(
            num_scalar_prefetch=1,
            grid=(steps,),
            in_specs=[
                pl.BlockSpec((rows, width), at),
                whole(vecs.shape),
                whole(wq.shape),
                whole(wk.shape),
                whole(wv.shape),
                pl.BlockSpec((rows, first.shape[1]), at),
            ],
            out_specs=(pl.BlockSpec((rows, width), out),) + (pl.BlockSpec((rows, cols), out),) * 4,
        ),
        compiler_params=params(),
        name="project",
    )(place, x, vecs, wq, wk, wv, first)


def span_bias(start, size, base, keys, rows, row0):
    key_pos = base + lax.broadcasted_iota(jnp.int32, (keys, rows), 0)
    query_pos = base + row0 + lax.broadcasted_iota(jnp.int32, (keys, rows), 1)
    stop = start + size
    both = (key_pos >= start) & (key_pos < stop) & (query_pos >= start) & (query_pos < stop)
    return jnp.where((key_pos <= query_pos) | both, 0.0, far_below)


def in_tile(part, head, width):
    if width == HD:
        return part
    zero = jnp.zeros_like(part)
    return jnp.concatenate([part, zero] if head % 2 == 0 else [zero, part], 0)


def store_half(side, half, rows, value, own_ref, other_ref):
    @pl.when(side == half)
    def _():
        own_ref[rows, :] = value

    @pl.when(side != half)
    def _():
        other_ref[rows, :] = value


def attend_body(place, start, size, q_ref, k_ref, v_ref, *rest, heads, span, rb, last):
    if last:
        low_ref, wq_ref, wk_ref, zt0_ref, wo0_ref, wo_ref, zt_ref, lse_ref, q_out, k_out, own_ref, other_ref, bias_ref = rest
        q_out[...] = nt(low_ref[...], wq_ref[...]).astype(BF16)
        k_out[...] = nt(low_ref[...], wk_ref[...]).astype(BF16)
        q_ref, k_ref = q_out, k_out
    else:
        zt_ref, lse_ref, bias_ref = rest
    length = q_ref.shape[0]
    lanes = heads * HD
    half = length // 2
    seq = place[CHIP]
    vt = v_ref[...].T
    qt = (q_ref[...] * score_scale).T
    for p in range(length // span):
        for r in range(0, span, rb):
            bias_ref[:, r : r + rb] = span_bias(start[seq, p], size[seq, p], p * span, span, rb, r)
        before = p * span
        keys = before + span
        for r in range(0, span, rb):
            row0 = before + r
            outs = []
            for h in range(heads):
                lo = h // 2 * 2 * HD
                hi = min(lo + 2 * HD, lanes)
                qh = in_tile(qt[h * HD : (h + 1) * HD, row0 : row0 + rb], h, hi - lo)
                vth = vt[h * HD : (h + 1) * HD, :]
                scores = nn(k_ref[:keys, lo:hi], qh)
                diag = scores[before:] + bias_ref[:, r : r + rb]
                peak = jnp.max(diag, axis=0, keepdims=True)
                if p:
                    peak = jnp.maximum(peak, jnp.max(scores[:before], axis=0, keepdims=True))
                raw = jnp.exp(diag - peak)
                total = jnp.sum(raw, axis=0, keepdims=True)
                zt = nn(vth[:, before:keys], raw.astype(BF16))
                if p:
                    raw = jnp.exp(scores[:before] - peak)
                    total = total + jnp.sum(raw, axis=0, keepdims=True)
                    zt = zt + nn(vth[:, :before], raw.astype(BF16))
                outs.append((zt / total).astype(BF16))
                lse_ref[h : h + 1, row0 : row0 + rb] = peak + jnp.log(total)
            zt = jnp.concatenate(outs, 0)
            zt_ref[:, row0 : row0 + rb] = zt
            if last:
                out = nn(zt.T, wo_ref[...]) + nn(zt0_ref[:, row0 : row0 + rb].T, wo0_ref[...])
                at = row0 % half
                store_half(place[CORE], row0 // half, slice(at, at + rb), out.astype(BF16), own_ref, other_ref)


def attend(place, start, size, q, k, v, more, heads, rb=512):
    length, lanes = v.shape
    span = length // start.shape[1]
    rb = min(rb, span, length // 2)
    outs = [shaped((lanes, length), BF16), shaped((heads, length), F32)]
    if more:
        width = more[-1].shape[1]
        outs += [shaped(v.shape, BF16)] * 2 + [shaped((length // 2, width), BF16)] * 2
    ins = (q, k, v) + tuple(more)
    return pl.pallas_call(
        partial(attend_body, heads=heads, span=span, rb=rb, last=bool(more)),
        out_shape=tuple(outs),
        grid_spec=pltpu.PrefetchScalarGridSpec(
            num_scalar_prefetch=3,
            grid=(1,),
            in_specs=[whole(i.shape) for i in ins],
            out_specs=tuple(whole(o.shape) for o in outs),
            scratch_shapes=[pltpu.VMEM((span, span), F32)],
        ),
        compiler_params=params(),
        name="attend_out" if more else "attend",
    )(place, start, size, *ins)


def attend_pull_body(
    place, start, size, q_ref, k_ref, v_ref, wo_ref, zt_ref, lse_ref, own_in, other_in, low_ref, *rest,
    heads, span, rb, last,
):
    if last:
        (wq_ref, wk_ref, wq0_ref, wk0_ref, wv_ref, dqt0_ref, dk0_ref, dv0_ref, grad_ref, own_ref, other_ref, first_ref,
         bias_ref, dk_sum, dv_sum, dqt_ref, dh_ref) = rest
    else:
        grad_ref, dqt_ref, dk_ref, dv_ref, bias_ref, dk_sum, dv_sum, dh_ref = rest
    length, lanes = q_ref.shape
    half = length // 2
    seq = place[CHIP]
    left = place[CORE] == 0
    dh_ref[:half, :] = jnp.where(left, own_in[...], other_in[...])
    dh_ref[half:, :] = jnp.where(left, other_in[...], own_in[...])
    dz = nt(dh_ref[...], wo_ref[...]).astype(BF16)
    dzt = dz.T
    q = q_ref[...] * score_scale
    qt = q.T
    kt = k_ref[...].T
    low_lane = lax.broadcasted_iota(jnp.int32, (1, 2 * HD), 1) < HD
    dk_sum[...] = jnp.zeros_like(dk_sum)
    dv_sum[...] = jnp.zeros_like(dv_sum)
    for p in range(length // span):
        for r in range(0, span, rb):
            bias_ref[:, r : r + rb] = span_bias(start[seq, p], size[seq, p], p * span, span, rb, r)
        before = p * span
        keys = before + span
        for r in range(0, span, rb):
            row0 = before + r
            dqs = []
            for lo in range(0, lanes, 2 * HD):
                hi = min(lo + 2 * HD, lanes)
                dks = []
                dvs = []
                for h in range(lo // HD, hi // HD):
                    qh = in_tile(qt[h * HD : (h + 1) * HD, row0 : row0 + rb], h, hi - lo)
                    dzh = in_tile(dzt[h * HD : (h + 1) * HD, row0 : row0 + rb], h, hi - lo)
                    lse = lse_ref[h : h + 1, row0 : row0 + rb]
                    scores = nn(k_ref[:keys, lo:hi], qh)
                    dprob = nn(v_ref[:keys, lo:hi], dzh)
                    prob = jnp.exp(scores[before:] + bias_ref[:, r : r + rb] - lse)
                    both = prob * dprob[before:]
                    delta = jnp.sum(both, axis=0, keepdims=True)
                    if p:
                        prob2 = jnp.exp(scores[:before] - lse)
                        both2 = prob2 * dprob[:before]
                        delta = delta + jnp.sum(both2, axis=0, keepdims=True)
                        prob_low = jnp.concatenate([prob2.astype(BF16), prob.astype(BF16)], 0)
                        ds = jnp.concatenate(
                            [(both2 - prob2 * delta).astype(BF16), (both - prob * delta).astype(BF16)], 0
                        )
                    else:
                        prob_low = prob.astype(BF16)
                        ds = (both - prob * delta).astype(BF16)
                    dqs.append((nn(kt[h * HD : (h + 1) * HD, :keys], ds) * score_scale).astype(BF16))
                    dks.append(nn(ds, q[row0 : row0 + rb, lo:hi]))
                    dvs.append(nn(prob_low, dz[row0 : row0 + rb, lo:hi]))
                if len(dks) == 2:
                    dk_sum[:keys, lo:hi] += jnp.where(low_lane, dks[0], dks[1])
                    dv_sum[:keys, lo:hi] += jnp.where(low_lane, dvs[0], dvs[1])
                else:
                    dk_sum[:keys, lo:hi] += dks[0]
                    dv_sum[:keys, lo:hi] += dvs[0]
            dqt_ref[:, row0 : row0 + rb] = jnp.concatenate(dqs, 0)
    dqt = dqt_ref[...]
    dk = dk_sum[...].astype(BF16)
    dv = dv_sum[...].astype(BF16)
    low = low_ref[...]
    grad_ref[:lanes, :] = nn(dqt, low).astype(BF16)
    grad_ref[lanes : 2 * lanes, :] = nn(dk.T, low).astype(BF16)
    grad_ref[2 * lanes : 3 * lanes, :] = nn(zt_ref[...], dh_ref[...]).astype(BF16)
    if not last:
        dk_ref[...] = dk
        dv_ref[...] = dv
        return
    own_fresh = place[CHIP] == 0
    fresh = jnp.where(own_fresh, dv, dv0_ref[...])
    first_ref[...] = jnp.where(own_fresh, dv0_ref[...], dv)
    grad_ref[3 * lanes :, :] = nn(fresh.T, low).astype(BF16)
    wv = jnp.where(left, wv_ref[:, :lanes], wv_ref[:, lanes:])
    dx = nn(dqt.T, wq_ref[...]) + nn(dk, wk_ref[...]) + nt(fresh, wv)
    dx = dx + nn(dqt0_ref[...].T, wq0_ref[...]) + nn(dk0_ref[...], wk0_ref[...])
    dx = dx.astype(BF16)
    for part in range(2):
        store_half(place[CORE], part, slice(0, half), dx[part * half : (part + 1) * half], own_ref, other_ref)


def attend_pull(place, start, size, ins, more, heads, rb=256):
    q, own = ins[0], ins[6]
    length, lanes = q.shape
    width = own.shape[1]
    span = length // start.shape[1]
    rb = min(rb, span)
    ins = tuple(ins) + tuple(more)
    column = shaped((length, lanes), BF16)
    turned = shaped((lanes, length), BF16)
    scratch = [pltpu.VMEM((span, span), F32), pltpu.VMEM((length, lanes), F32), pltpu.VMEM((length, lanes), F32)]
    if more:
        outs = (shaped((4 * lanes, width), BF16), shaped(own.shape, BF16), shaped(own.shape, BF16), column)
        scratch.append(pltpu.VMEM((lanes, length), BF16))
    else:
        outs = (shaped((3 * lanes, width), BF16), turned, column, column)
    scratch.append(pltpu.VMEM((length, width), BF16))
    return pl.pallas_call(
        partial(attend_pull_body, heads=heads, span=span, rb=rb, last=bool(more)),
        out_shape=outs,
        grid_spec=pltpu.PrefetchScalarGridSpec(
            num_scalar_prefetch=3,
            grid=(1,),
            in_specs=[whole(i.shape) for i in ins],
            out_specs=tuple(whole(o.shape) for o in outs),
            scratch_shapes=scratch,
        ),
        compiler_params=params(),
        name="attend_pull_out" if more else "attend_pull",
    )(place, start, size, *ins)


def row_call(body, place, ins, outs, sums, rows, name):
    half = next(array.shape[0] for array, kind in ins if kind == "half")
    steps = half // rows
    specs = []
    for array, kind in ins:
        if kind == "half":
            specs.append(pl.BlockSpec((rows, array.shape[1]), lambda i, s: (i, 0)))
        elif kind == "all":
            specs.append(pl.BlockSpec((rows, array.shape[1]), lambda i, s: (s[0] * steps + i, 0)))
        else:
            specs.append(whole(array.shape))
    out_specs = [pl.BlockSpec((rows, o.shape[1]), lambda i, s: (i, 0)) for o in outs]
    out_specs += [whole(o.shape) for o in sums]
    return pl.pallas_call(
        body,
        out_shape=tuple(outs) + tuple(sums),
        grid_spec=pltpu.PrefetchScalarGridSpec(
            num_scalar_prefetch=1, grid=(steps,), in_specs=specs, out_specs=tuple(out_specs)
        ),
        compiler_params=params(),
        name=name,
    )(place, *[array for array, _ in ins])


def norm_mid_body(place, part_ref, got_ref, x_ref, vec_ref, hidden_ref, low_ref):
    hidden = x_ref[...].astype(F32) + (part_ref[...].astype(F32) + got_ref[...].astype(F32))
    hidden_ref[...] = hidden
    normal, _ = normal_parts(hidden)
    low_ref[...] = (normal * vec_ref[2:3, :] + vec_ref[3:4, :]).astype(BF16)


def add_sums(sum_ref, values):
    @pl.when(pl.program_id(0) == 0)
    def _():
        sum_ref[...] = jnp.zeros_like(sum_ref)

    for row, value in enumerate(values):
        sum_ref[row : row + 1, :] += jnp.sum(value, axis=0, keepdims=True)


def norm_mid_pull_body(place, part_ref, near_ref, far_ref, hidden_ref, cot_ref, vec_ref, dhidden_ref, low_ref, sum_ref):
    upstream = part_ref[...].astype(F32) + near_ref[...].astype(F32) + far_ref[...].astype(F32)
    normal, inverse = normal_parts(hidden_ref[...])
    cot = cot_ref[...].astype(F32)
    dhidden = cot + norm_pull(upstream, normal, inverse, vec_ref[2:3, :])
    dhidden_ref[...] = dhidden
    low_ref[...] = dhidden.astype(BF16)
    add_sums(sum_ref, (upstream * normal, upstream, cot))


def norm_first_pull_body(place, part_ref, got_ref, dhidden_ref, x_ref, vec_ref, out_ref, sum_ref):
    upstream = part_ref[...].astype(F32) + got_ref[...].astype(F32)
    normal, inverse = normal_parts(x_ref[...].astype(F32))
    out_ref[...] = (dhidden_ref[...] + norm_pull(upstream, normal, inverse, vec_ref[0:1, :])).astype(BF16)
    add_sums(sum_ref, (upstream * normal, upstream))


def output_body(place, hidden_ref, part_ref, near_ref, far_ref, vec_ref, out_ref):
    mlp = part_ref[...].astype(F32) + near_ref[...].astype(F32) + far_ref[...].astype(F32)
    out_ref[...] = (hidden_ref[...] + mlp + vec_ref[5:6, :]).astype(BF16)


def feed_body(place, x_ref, cot_ref, up_ref, vec_ref, down_ref, dx_ref, out_ref, active_ref, dpre_ref, sum_ref):
    pre = nn(x_ref[...], up_ref[...]) + vec_ref[4:5, :]
    root = 0.7978845608028654
    squared = pre * pre
    inner = jnp.tanh(root * pre * (1.0 + 0.044715 * squared))
    rise = 0.5 * (1.0 + inner)
    active = (pre * rise).astype(BF16)
    active_ref[...] = active
    slope = rise + 0.5 * pre * (1.0 - inner * inner) * (root * (1.0 + 3 * 0.044715 * squared))
    dpre = (nt(cot_ref[...], down_ref[...]) * slope).astype(BF16)
    dpre_ref[...] = dpre
    dx_ref[...] = nt(dpre, up_ref[...]).astype(BF16)
    out_ref[...] = nn(active, down_ref[...]).astype(BF16)
    add_sums(sum_ref, (dpre.astype(F32),))


def feed(place, x, cotangent, up, vecs, down, spot, rows=256):
    half, width = x.shape
    units = up.shape[1]
    steps = half // rows
    at = lambda i, s: (i, 0)
    cot_at = lambda i, s: (s[spot] * steps + i, 0)
    return pl.pallas_call(
        feed_body,
        out_shape=(
            shaped((half, width), BF16),
            shaped((half, width), BF16),
            shaped((half, units), BF16),
            shaped((half, units), BF16),
            shaped((1, units), F32),
        ),
        grid_spec=pltpu.PrefetchScalarGridSpec(
            num_scalar_prefetch=1,
            grid=(steps,),
            in_specs=[
                pl.BlockSpec((rows, width), at),
                pl.BlockSpec((rows, width), cot_at),
                whole(up.shape),
                whole(vecs.shape),
                whole(down.shape),
            ],
            out_specs=(
                pl.BlockSpec((rows, width), at),
                pl.BlockSpec((rows, width), at),
                pl.BlockSpec((rows, units), at),
                pl.BlockSpec((rows, units), at),
                whole((1, units)),
            ),
        ),
        compiler_params=params(),
        name="feed",
    )(place, x, cotangent, up, vecs, down)


def outer_body(place, *refs, count):
    total = tn(refs[0][...], refs[count][...])
    for i in range(1, count):
        total = total + tn(refs[i][...], refs[count + i][...])
    refs[-1][...] = total.astype(BF16)


def outer_sum(place, lefts, rights, spots=None):
    count = len(lefts)
    half, rows = lefts[0].shape
    cols = rights[0].shape[1]
    specs = [whole(a.shape) for a in lefts]
    for i in range(count):
        if spots is None:
            specs.append(whole(rights[i].shape))
        else:
            specs.append(pl.BlockSpec((half, cols), lambda _, s, spot=spots[i]: (s[spot], 0)))
    return pl.pallas_call(
        partial(outer_body, count=count),
        out_shape=shaped((rows, cols), BF16),
        grid_spec=pltpu.PrefetchScalarGridSpec(
            num_scalar_prefetch=1, grid=(1,), in_specs=specs, out_specs=whole((rows, cols))
        ),
        compiler_params=params(),
        name="outer_sum",
    )(place, *lefts, *rights)


def xor_pairs(size, bit):
    return [(i, i ^ bit) for i in range(size)]


def bits_of(size):
    return [1 << i for i in range(size.bit_length() - 1)]


def xor_sum(value, axis):
    size = lax.axis_size(axis)
    for bit in bits_of(size):
        value = value + lax.ppermute(value, axis, xor_pairs(size, bit))
    return value


def split_sum(value, axis):
    size = lax.axis_size(axis)
    place = lax.axis_index(axis)
    for bit in bits_of(size):
        half = value.shape[0] // 2
        mine = (place // bit) % 2
        away = lax.dynamic_slice_in_dim(value, (1 - mine) * half, half, 0)
        keep = lax.dynamic_slice_in_dim(value, mine * half, half, 0)
        got = lax.ppermute(away, axis, xor_pairs(size, bit))
        value = (keep.astype(F32) + got.astype(F32)).astype(value.dtype)
    for bit in reversed(bits_of(size)):
        got = lax.ppermute(value, axis, xor_pairs(size, bit))
        value = side_by_side((place // bit) % 2 == 0, value, got, 0)
    return value


def side_by_side(first, own, got, axis):
    return jnp.concatenate([jnp.where(first, own, got), jnp.where(first, got, own)], axis)


def on_device(
    inputs,
    first_values,
    piece_start,
    piece_length,
    cotangent,
    pre_attn_gain,
    pre_attn_bias,
    w_query,
    w_key,
    w_value,
    w_out,
    pre_mlp_gain,
    pre_mlp_bias,
    w_up,
    b_up,
    w_down,
    b_down,
):
    groups = lax.axis_size("tensor")
    member = lax.axis_index("tensor").astype(jnp.int32)
    heads = HEADS // groups
    lanes = heads * HD
    core = member % 2
    chip = member // 2
    tokens_dev, width = inputs.shape
    seq_count = piece_start.shape[0]
    assert groups == 4 and seq_count == 2
    length = tokens_dev // seq_count
    half = length // 2
    place = jnp.stack(
        [2 * chip + core, 2 * chip + 1 - core, 2 * (1 - chip) + core, 2 * (1 - chip) + 1 - core, chip, core]
    )
    near = partial(lax.ppermute, axis_name="tensor", perm=xor_pairs(groups, 1))
    far = partial(lax.ppermute, axis_name="tensor", perm=xor_pairs(groups, 2))

    wq, wk = w_query.T, w_key.T
    wq0, wk0, wo0 = far(wq), far(wk), far(w_out)
    vecs = jnp.stack([pre_attn_gain, pre_attn_bias, pre_mlp_gain, pre_mlp_bias, b_up, b_down, b_down, b_down])

    low, q, k, v, v0 = project(place, inputs, vecs, wq, wk, w_value, first_values, length)
    zt, lse = attend(place, piece_start, piece_length, q, k, v, (), heads)
    zt0, lse0, q0, k0, own, other = attend(
        place, piece_start, piece_length, q, k, v0, (low, wq0, wk0, zt, w_out, wo0), heads
    )
    hidden, mid = row_call(
        norm_mid_body,
        place,
        [(own, "half"), (near(other), "half"), (inputs, "all"), (vecs, "vector")],
        [shaped((half, width), F32), shaped((half, width), BF16)],
        [],
        128,
        "norm_mid",
    )
    mid_far = far(mid)
    mids = [mid, near(mid), mid_far, near(mid_far)]
    dmids, outs, acts, dpres, up_sums = zip(
        *[feed(place, mids[i], cotangent, w_up, vecs, w_down, i) for i in range(4)]
    )

    def pair_add(mine, got):
        return (mine.astype(F32) + got.astype(F32)).astype(BF16)

    dmid_far = far(pair_add(dmids[2], near(dmids[3])))
    dhidden, dlow, mid_sums = row_call(
        norm_mid_pull_body,
        place,
        [(dmids[0], "half"), (near(dmids[1]), "half"), (dmid_far, "half"), (hidden, "half"), (cotangent, "all"),
         (vecs, "vector")],
        [shaped((half, width), F32), shaped((half, width), BF16)],
        [shaped((3, width), F32)],
        128,
        "norm_mid_pull",
    )
    dlow_near = near(dlow)
    grads0, dqt0, dk0, dv0 = attend_pull(
        place, piece_start, piece_length, (q0, k0, v0, wo0, zt0, lse0, dlow, dlow_near, low), (), heads
    )
    grads0 = far(grads0)
    grads, own, other, dfirst = attend_pull(
        place, piece_start, piece_length, (q, k, v, w_out, zt, lse, dlow, dlow_near, low),
        (wq, wk, wq0, wk0, w_value, dqt0, dk0, dv0), heads,
    )
    grad_rows, first_sums = row_call(
        norm_first_pull_body,
        place,
        [(own, "half"), (near(other), "half"), (dhidden, "half"), (inputs, "all"), (vecs, "vector")],
        [shaped((half, width), BF16)],
        [shaped((2, width), F32)],
        128,
        "norm_first_pull",
    )

    grad_w_down = split_sum(outer_sum(place, acts, [cotangent] * 4, range(4)), "dp").astype(F32)
    grad_w_up = split_sum(outer_sum(place, mids, dpres), "dp").astype(F32)

    out_far = far(pair_add(outs[2], near(outs[3])))
    (out_rows,) = row_call(
        output_body,
        place,
        [(hidden, "half"), (outs[0], "half"), (near(outs[1]), "half"), (out_far, "half"), (vecs, "vector")],
        [shaped((half, width), BF16)],
        [],
        256,
        "output",
    )

    def everywhere(rows):
        rows_far = far(rows)
        mine = side_by_side(core == 0, rows, near(rows), 0)
        theirs = side_by_side(core == 0, rows_far, near(rows_far), 0)
        return side_by_side(chip == 0, mine, theirs, 0)

    outputs = everywhere(out_rows)
    grad_inputs = everywhere(grad_rows).astype(F32)

    dfirst_far = far(dfirst)
    grad_first_values = side_by_side(
        chip == 0,
        side_by_side(core == 0, dfirst, near(dfirst), 1),
        side_by_side(core == 0, dfirst_far, near(dfirst_far), 1),
        0,
    ).astype(F32)

    grads = jnp.concatenate([grads0, far(grads[3 * lanes :])], 0).astype(F32) + grads.astype(F32)
    grads = split_sum(grads.astype(BF16), "dp")
    gv = grads[3 * lanes :]
    grad_w_value = side_by_side(core == 0, gv, near(gv), 0).T.astype(F32)

    mid_sums = mid_sums + near(mid_sums)
    mid_sums = mid_sums + far(mid_sums)
    mid_sums = xor_sum(jnp.concatenate([mid_sums, sum(up_sums)], 0), "dp")
    first_sums = first_sums + near(first_sums)
    first_sums = first_sums + far(first_sums)
    first_sums = xor_sum(first_sums, "dp")

    return (
        outputs,
        grad_inputs,
        grad_first_values,
        first_sums[0],
        first_sums[1],
        grads[:lanes].T.astype(F32),
        grads[lanes : 2 * lanes].T.astype(F32),
        grad_w_value,
        grads[2 * lanes : 3 * lanes].astype(F32),
        mid_sums[0],
        mid_sums[1],
        grad_w_up,
        mid_sums[3],
        grad_w_down,
        mid_sums[2],
    )


def solution(mesh):
    return jax.shard_map(
        on_device,
        mesh=mesh,
        in_specs=(
            P("dp", None),
            P("dp", None),
            P("dp", None),
            P("dp", None),
            P("dp", None),
            P(),
            P(),
            P(None, "tensor"),
            P(None, "tensor"),
            P(),
            P("tensor", None),
            P(),
            P(),
            P(None, "tensor"),
            P("tensor"),
            P("tensor", None),
            P(),
        ),
        out_specs=(
            P("dp", None),
            P("dp", None),
            P("dp", None),
            P(),
            P(),
            P(None, "tensor"),
            P(None, "tensor"),
            P(),
            P("tensor", None),
            P(),
            P(),
            P(None, "tensor"),
            P("tensor"),
            P("tensor", None),
            P(),
        ),
        check_vma=False,
    )
```
